128 devices in a mesh: tm: 32 (over z, y, core), clus: 4 (over x).
Axes of the slice: x: 4, y: 4, z: 4, core: 2. Of those that a mesh axis runs over, the one named last changes fastest.
Arguments:
- right_side: float32 [15, 131072], P(None, ('tm', 'clus')), may hold values from -8 to 8
- transition: float32 [15, 15, 131072], P(None, None, ('tm', 'clus')), may hold values from -1.5 to 1.5
- precond: float32 [15, 15, 131072], P(None, None, ('tm', 'clus')), as said below
- slot_of: int32 [131072], P(('tm', 'clus')), may hold values from 0 to 1023, as said below
- cluster_id: int32 [32, 4096], P('tm', 'clus'), may hold values from 0 to 63, never falling along the last dimension, each value on 1 to 128 neighbouring positions
- damping: float32 [32, 64], P('tm'), may hold values from 0.3 to 3
- pair_first: int32 [32, 8192], P('tm', 'clus'), may hold values from 0 to 4095
- pair_second: int32 [32, 8192], P('tm', 'clus'), may hold values from 0 to 4095
- pair_blocks: float32 [15, 15, 32, 8192], P(None, None, 'tm', 'clus'), may hold values from -1.5 to 1.5
Outputs:
- solution_field: float32 [15, 131072], P(None, ('tm', 'clus'))
- residual: float32 [15, 131072], P(None, ('tm', 'clus'))
The draws below stay inside these ranges and needn't reach their ends.
Inputs may be any that keep to these rules, and one draw needn't show every extreme that they name: `slot_of`: the 1024 entries of each device's block are a permutation of 0 to 1023. `cluster_id`: never falling along each group's keyframes. `precond`: each keyframe's block is symmetric positive definite.
All inputs are finite; a program needn't handle non-finite values.
Results may differ from the reference program's by a relative error of at most 0.00015.
Values sent between devices are 32-bit elements; how exact they have to be, the bound alone decides.
A program may use at most 128 MiB of HBM per device.

```python
import math
import jax
import jax.numpy as jnp
import numpy as np
from jax import lax

STATE = 15
KF_DEV = 1024
CLUSTERS = 64
ITERS = 2
KEYFRAMES = 131072
GROUP_KF = 4096
PAIR_GROUP = 8192
N_TM = 32
N_CLUS = 4


def draw_precond(key, part):
    first, second = jax.random.split(key)
    diag = jnp.exp(jax.random.uniform(first, (STATE, KEYFRAMES), jnp.float32, jnp.log(0.5), jnp.log(4.0)))
    noise = jax.random.uniform(second, (STATE, STATE, KEYFRAMES), jnp.float32, -1.0, 1.0)
    eye = jnp.eye(STATE, dtype=jnp.float32)
    sym = (noise + jnp.transpose(noise, (1, 0, 2))) * 0.0175 * (1.0 - eye)[:, :, None]
    return sym + eye[:, :, None] * diag[:, None, :]


def draw_slot_of(key, part):
    blocks = KEYFRAMES // KF_DEV
    keys = jax.random.split(key, blocks)
    perms = jax.vmap(lambda one: jax.random.permutation(one, KF_DEV))(keys)
    return perms.reshape(-1).astype(jnp.int32)


def set_ends(drawn, stream_key, low, top_value):
    spot = [jax.random.randint(jax.random.fold_in(stream_key, axis), (), 0, length) for axis, length in enumerate(drawn.shape)]
    widest = drawn.shape.index(max(drawn.shape))
    next_to = spot[:widest] + [(spot[widest] + 1) % drawn.shape[widest]] + spot[widest + 1:]
    return drawn.at[tuple(spot)].set(low).at[tuple(next_to)].set(top_value)


def block_scale(key, shape, cuts, smallest, top_value):
    factor_of, own = 1.0, jax.random.fold_in(key, 6)
    for position, parts in cuts:
        draws = jnp.exp(jax.random.uniform(jax.random.fold_in(own, position), (parts,), jnp.float32, smallest / len(cuts), top_value / len(cuts)))
        factor_of = factor_of * jnp.repeat(draws, shape[position] // parts).reshape([-1 if axis == position else 1 for axis in range(len(shape))])
    return factor_of


def profile(count, total, most, slope):
    portions = [(1 << 20) // math.isqrt(rank ** slope) + 1 for rank in range(2, count + 1)]
    spare, holding = total - most - (count - 1), [1] * (count - 1)
    while spare > 0:
        free = [i for i in range(count - 1) if holding[i] < most]
        mass, budget = sum([portions[i] for i in free]), spare
        for i in free:
            addition = min(most - holding[i], max(1, budget * portions[i] // mass), spare)
            holding[i] = holding[i] + addition
            spare = spare - addition
    return np.array([most] + holding)


def uneven_parts(rng, count, total, most, skew):
    if count == 2:
        one = jax.random.randint(rng, (), max(1, total - most), min(most, total - 1) + 1)
        return jnp.stack([one, total - one])
    lengths = jnp.asarray(profile(count, total, most, skew), jnp.int32)
    couples = (count - 1) // 2
    giver, taker = lengths[1:1 + 2 * couples:2], lengths[2:2 + 2 * couples:2]
    margin = jnp.minimum(giver - 1, most - taker)
    passed = jax.random.randint(jax.random.fold_in(rng, 1), (couples,), 0, 1 << 20) % (margin + 1)
    lengths = lengths.at[1:1 + 2 * couples:2].set(giver - passed).at[2:2 + 2 * couples:2].set(taker + passed)
    return lengths[jax.random.permutation(jax.random.fold_in(rng, 2), count)]


def scatter_about(own_key, extent, width, reach, pieces=(), kind=jnp.bfloat16):
    entries = jax.random.normal(own_key, extent, jnp.float32) * width
    if len(pieces) > 0:
        entries = block_scale(own_key, extent, pieces, -0.22, 0.18) * entries
    return jnp.clip(entries, min=-reach, max=reach).astype(kind)


def setup_inputs(seed: int = 0) -> dict:
    key_of = jax.random.split(jax.random.key(seed), 10)
    return {
        "right_side": scatter_about(key_of[0], (STATE, KEYFRAMES), 1.0, 8.0, ((1, 128),), jnp.float32),
        "transition": scatter_about(key_of[1], (STATE, STATE, KEYFRAMES), STATE ** -0.5, 1.5, ((2, 128),), jnp.float32),
        "precond": draw_precond(jax.random.fold_in(key_of[9], 71), 0),
        "slot_of": draw_slot_of(jax.random.fold_in(key_of[9], 71), 0),
        "cluster_id": jax.vmap(lambda own: jnp.searchsorted(jnp.cumsum(uneven_parts(own, CLUSTERS, GROUP_KF, 2 * GROUP_KF // CLUSTERS, 1)), jnp.arange(GROUP_KF), side="right"))(jax.random.split(key_of[4], N_TM)).reshape((N_TM, GROUP_KF)).astype(jnp.int32),
        "damping": jnp.clip(jnp.exp(math.log(3.0) - 2.3025851 * jax.random.uniform(key_of[5], (N_TM, CLUSTERS), jnp.float32) ** block_scale(key_of[5], (N_TM, CLUSTERS), ((0, 32),), -0.2, 0.2)), 0.3, 3.0),
        "pair_first": set_ends(jax.random.randint(key_of[6], (N_TM, PAIR_GROUP), 0, GROUP_KF), jax.random.fold_in(key_of[6], 1), 0, GROUP_KF - 1).astype(jnp.int32),
        "pair_second": set_ends(jax.random.randint(key_of[7], (N_TM, PAIR_GROUP), 0, GROUP_KF), jax.random.fold_in(key_of[7], 1), 0, GROUP_KF - 1).astype(jnp.int32),
        "pair_blocks": scatter_about(key_of[8], (STATE, STATE, N_TM, PAIR_GROUP), STATE ** -0.5, 1.5, ((2, 32), (3, 4)), jnp.float32),
    }


def inertial(field, transition):
    total = field.shape[1]
    moved = jnp.einsum('ijk,jk->ik', transition, field, precision=lax.Precision.HIGHEST)
    following = jnp.concatenate([field[:, 1:], jnp.zeros((field.shape[0], 1), field.dtype)], axis=1)
    keep = jnp.where(jnp.arange(total) < total - 1, 1.0, 0.0).astype(field.dtype)
    errors = (following - moved) * keep[None, :]
    back = jnp.einsum('jik,jk->ik', transition, errors, precision=lax.Precision.HIGHEST)
    earlier = jnp.concatenate([jnp.zeros((field.shape[0], 1), field.dtype), errors[:, :-1]], axis=1)
    return earlier - back


def positions(slot_of):
    share = KF_DEV // N_TM
    index = jnp.arange(KEYFRAMES).astype(jnp.int32)
    block = index // KF_DEV
    tpos = block // N_CLUS
    cpos = block % N_CLUS
    group = slot_of // share
    inner = slot_of % share
    return ((group * N_CLUS + cpos) * KF_DEV + tpos * share + inner).astype(jnp.int32)


def visual(field, place, cluster_id, damping, pair_first, pair_second, pair_blocks):
    clustered = jnp.zeros_like(field).at[:, place].set(field)
    offsets = (jnp.arange(N_TM).astype(jnp.int32) * GROUP_KF)[:, None]
    heads = (pair_first + offsets).reshape(-1)
    tails = (pair_second + offsets).reshape(-1)
    blocks = pair_blocks.reshape(pair_blocks.shape[0], pair_blocks.shape[1], -1)
    near = jnp.take(clustered, heads, axis=1)
    far = jnp.take(clustered, tails, axis=1)
    errors = near - jnp.einsum('ijp,jp->ip', blocks, far, precision=lax.Precision.HIGHEST)
    back = jnp.einsum('jip,jp->ip', blocks, errors, precision=lax.Precision.HIGHEST)
    lam = jnp.take_along_axis(damping, cluster_id, axis=1).reshape(-1)
    image = jnp.zeros_like(field).at[:, heads].add(errors).at[:, tails].add(-back) + lam[None, :] * clustered
    return jnp.take(image, place, axis=1)


def reference(right_side, transition, precond, slot_of, cluster_id, damping, pair_first, pair_second, pair_blocks):
    place = positions(slot_of)

    def apply(field):
        return inertial(field, transition) + visual(field, place, cluster_id, damping, pair_first, pair_second, pair_blocks)

    def condition(field):
        return jnp.einsum('ijk,jk->ik', precond, field, precision=lax.Precision.HIGHEST)

    solution_field = jnp.zeros_like(right_side)
    residual = right_side
    scaled = condition(residual)
    direction = scaled
    rz_now = jnp.sum(residual * scaled)
    for step in range(ITERS):
        image = apply(direction)
        alpha = rz_now / jnp.sum(direction * image)
        solution_field = solution_field + alpha * direction
        residual = residual - alpha * image
        scaled = condition(residual)
        rz_next = jnp.sum(residual * scaled)
        direction = scaled + (rz_next / rz_now) * direction
        rz_now = rz_next
    return solution_field, residual
```

```python
import jax
import jax.numpy as jnp
from jax import lax
from jax.experimental import pallas as pl
from jax.experimental.pallas import tpu as pltpu
from jax.sharding import PartitionSpec as P

MESHID = pl.DeviceIdType.MESH
F32 = jnp.float32
BF16 = jnp.bfloat16
N = 15


def hops(d):
    return min(d, 4 - d)


RINGS = sorted(((z, y) for z in range(4) for y in range(4)), key=lambda a: -hops(a[0]) - hops(a[1]))


def sweep(action):
    tm = lax.axis_index("tm")
    cl = lax.axis_index("clus")
    z, y, core = tm // 8, (tm // 2) % 4, tm % 2
    for dz, dy in RINGS:
        row = ((z + dz) % 4) * 8 + ((y + dy) % 4) * 2
        first = 1 if (dz, dy) == (0, 0) else 0

        def one(i, c):
            action(row + (core + i // 4) % 2, (cl + i % 4) % 4)
            return c

        lax.fori_loop(first, 8, one, 0)


def iota(shape, axis):
    return lax.broadcasted_iota(jnp.int32, shape, axis)


def total(v):
    while v.ndim > 2:
        v = jnp.sum(v, axis=0)
    return jnp.sum(v, axis=(0, 1), keepdims=True)


def loop(n, body):
    def step(i, c):
        body(i)
        return c

    lax.fori_loop(0, n, step, 0)


def rows8(i):
    return pl.ds(pl.multiple_of(i * 8, 8), 8)


def rows16(i):
    return pl.ds(pl.multiple_of(i * 16, 16), 16)


def rows4(i):
    return pl.ds(pl.multiple_of(i * 4, 4), 4)


def lanes(i):
    return pl.ds(pl.multiple_of(i * 128, 128), 128)


def multiply(blocks, src, dst):
    field = src[0:120, :].reshape(N, 8, 128)

    def one(i):
        dst[rows8(i), :] = jnp.sum(blocks[i] * field, axis=0)

    loop(N, one)


def after(v):
    turned = pltpu.roll(v, 127, axis=1)
    return jnp.where(iota((8, 128), 1) == 127, pltpu.roll(turned, 7, axis=0), turned)


def before(v):
    turned = pltpu.roll(v, 1, axis=1)
    return jnp.where(iota((8, 128), 1) == 0, pltpu.roll(turned, 1, axis=0), turned)


def spread(row, j):
    return jnp.take_along_axis(jnp.broadcast_to(row, (8, 128)), jnp.full((8, 128), j, jnp.int32), axis=1)


def extras(z2, mv2, scalar):
    lane, sub = iota((16, 128), 1), iota((16, 128), 0)
    first = jnp.sum(jnp.where(lane == 0, z2[pl.ds(0, 16, stride=8), :], 0.0), axis=1, keepdims=True)
    last = jnp.sum(jnp.where(lane == 127, mv2[pl.ds(7, 16, stride=8), :], 0.0), axis=1, keepdims=True)
    row = jnp.where(lane % 32 == sub, first, 0.0) + jnp.where(lane % 32 == sub + N, last, 0.0)
    return jnp.where(iota((1, 128), 1) % 32 == 30, scalar, jnp.sum(row, axis=0, keepdims=True))


def fill(src2, stride, tiles, base, count, onehot, lhs):
    def one(a):
        v = src2[pl.ds(a, 16, stride=stride), :]
        high = v.astype(BF16)
        low = (v - high.astype(F32)).astype(BF16)
        cols = lanes(base + a)
        for n in range(count):
            mask = onehot[n * 16 : (n + 1) * 16, cols]
            lhs[0, n * 16 : (n + 1) * 16, cols] = high * mask
            lhs[1, n * 16 : (n + 1) * 16, cols] = low * mask

    loop(tiles, one)


def spread_sum(lhs, wt, sums, count):
    dims = (((1,), (1,)), ((), ()))
    made = lax.dot_general(lhs[0], wt[...], dims, preferred_element_type=F32) + lax.dot_general(
        lhs[1], wt[...], dims, preferred_element_type=F32
    )
    sums[0, 0:count, :] = made[:, 0:128]
    sums[1, 0:count, :] = made[:, 128:256]


def messages(sums, count, row, out):
    for half in range(2):
        sums[half, pl.ds(N, count, stride=16), :] = jnp.broadcast_to(row, (count, 128))
    group = iota((8, 128), 1) // 32

    def one(hp):
        for half in range(2):
            made = [None] * 4
            for jj in range(4):
                v = sums[half, pl.ds(hp * 32 + jj, 8, stride=4), :]
                for tl in range(4):
                    turn = ((jj - tl) % 4) * 32
                    moved = pltpu.roll(v, turn, axis=1) if turn else v
                    made[tl] = moved if jj == 0 else jnp.where(group == jj, moved, made[tl])
            for tl in range(4):
                out[half * 4 + tl, rows8(hp), :] = made[tl]

    loop(count // 2, one)


def regroup(parts, jj):
    group = iota((8, 128), 1) // 32
    made = None
    for tl in range(4):
        turn = ((tl - jj) % 4) * 32
        moved = pltpu.roll(parts[tl], turn, axis=1) if turn else parts[tl]
        made = moved if tl == 0 else jnp.where(group == tl, moved, made)
    return made


def scalar_of(v):
    keep = (iota(v.shape, 0) % 4 == 3) & (iota(v.shape, 1) % 32 == 30)
    return total(jnp.where(keep, v, 0.0))


def kernel(
    b_ref, slot_row, slot8, cid8, damp_ref, pf_row, ps_row, pf16, ps16, m_any, t_any, blk_any,
    x_out, r_out,
    mb, tb, blk, r2, z2, d2, mv, mvd, e2, jv, x2, near, far, f2, b2, tab, tab2, sums,
    wt_s, oh_s, lhs_s, wt_p, oh_p, lhs_p, lam, out_f, out_b, recv_f, recv_b,
    load_sem, send_sem, recv_sem,
):
    tm = lax.axis_index("tm")
    cl = lax.axis_index("clus")
    flat = tm * 4 + cl
    bar = pltpu.get_barrier_semaphore()
    sweep(lambda t, c: pl.semaphore_signal(bar, 1, device_id=(t, c), device_id_type=MESHID))

    loads = []
    for n, (src, dst) in enumerate(((m_any, mb), (t_any, tb))):
        loads.append(
            [pltpu.make_async_copy(src.at[:, :, pl.ds(a * 128, 128)], dst.at[:, :, a, :], load_sem.at[n, a]) for a in range(8)]
        )
    loads.append([pltpu.make_async_copy(blk_any, blk, load_sem.at[2, 0])])
    for group in loads:
        for copy in group:
            copy.start()

    r2[...] = jnp.zeros_like(r2)
    z2[120:128, :] = jnp.zeros((8, 128), F32)
    mv[120:128, :] = jnp.zeros((8, 128), F32)
    f2[240:256, :] = jnp.zeros((16, 128), F32)
    b2[240:256, :] = jnp.zeros((16, 128), F32)
    for a in range(8):
        r2[pl.ds(a, N, stride=8), :] = b_ref[:, a * 128 : (a + 1) * 128]

    def slots(a):
        index = slot_row[:, lanes(a)]
        wt_s[:, lanes(a)] = jnp.where(iota((256, 128), 0) == index % 256, 1.0, 0.0).astype(BF16)
        oh_s[:, lanes(a)] = jnp.where(iota((64, 128), 0) // 16 == index // 256, 1.0, 0.0).astype(BF16)

    loop(8, slots)

    pos_first = (iota((8, 128), 0) == 0) & (iota((8, 128), 1) == 0)
    pos_last = (iota((8, 128), 0) == 7) & (iota((8, 128), 1) == 127)
    keep_last = jnp.where(pos_last & (flat == 127), 0.0, 1.0)
    keep_first = jnp.where(pos_first & (flat == 0), 0.0, 1.0)
    following, previous = (flat + 1) % 128, (flat + 127) % 128

    def halo(ph, who):
        return recv_f[ph, (who // 4) % 8, pl.ds(((who % 4) * 4 + who // 32) * 4 + 3, 1), :]

    rz = None
    for ph in range(2):
        if ph == 0:
            for copy in loads[0]:
                copy.wait()
        multiply(mb, r2, z2)
        part = total((r2[0:120, :] * z2[0:120, :]).reshape(N, 8, 128))
        if ph == 0:
            for copy in loads[1]:
                copy.wait()
        multiply(tb, z2, mv)
        row = extras(z2, mv, part)
        fill(z2, 8, 8, 0, 4, oh_s, lhs_s)
        spread_sum(lhs_s, wt_s, sums, 64)
        messages(sums, 4, row, out_f.at[ph])
        if ph == 0:
            pl.semaphore_wait(bar, 127)

        def send_f(t, c):
            pltpu.make_async_remote_copy(
                out_f.at[ph, t % 8, rows4(t // 8), :],
                recv_f.at[ph, tm % 8, rows4(cl * 4 + tm // 8), :],
                send_sem.at[ph, 0],
                recv_sem.at[ph, 0],
                device_id=(t, c),
                device_id_type=MESHID,
            ).start()

        sweep(send_f)
        pltpu.make_async_copy(
            out_f.at[ph, tm % 8, rows4(tm // 8), :], recv_f.at[ph, tm % 8, rows4(cl * 4 + tm // 8), :], recv_sem.at[ph, 0]
        ).start()

        if ph == 0:

            def pairs(a):
                for base, ref in ((0, pf_row), (16, ps_row)):
                    index = ref[:, lanes(a)]
                    wt_p[:, lanes(base + a)] = jnp.where(iota((256, 128), 0) == index % 256, 1.0, 0.0).astype(BF16)
                    oh_p[:, lanes(base + a)] = jnp.where(iota((256, 128), 0) // 16 == index // 256, 1.0, 0.0).astype(BF16)

            loop(16, pairs)
            per = jnp.take_along_axis(jnp.broadcast_to(damp_ref[...], (8, 128)), cid8[...], axis=1)
            group = iota((8, 128), 1) // 32
            spare = (iota((4, 128), 0) == 3) & (iota((4, 128), 1) >= 96)
            for tl in range(4):
                wide = None
                for jj in range(4):
                    turn = ((jj - tl) % 4) * 32
                    moved = pltpu.roll(per, turn, axis=1) if turn else per
                    wide = moved if jj == 0 else jnp.where(group == jj, moved, wide)
                for t4 in range(8):
                    th, h = t4 // 2, t4 % 2
                    lam[h * 4 + tl, th * 4 : (th + 1) * 4, :] = jnp.where(spare, 0.0, jnp.broadcast_to(wide[t4 : t4 + 1, :], (4, 128)))
            loads[2][0].wait()

        pltpu.make_async_copy(recv_f.at[ph], recv_f.at[ph], recv_sem.at[ph, 0]).wait()

        def tables(hp):
            for h in range(2):
                parts = [recv_f[ph, h * 4 + tl, rows8(hp), :] for tl in range(4)]
                for jj in range(4):
                    tab[jj, h, rows8(hp), :] = regroup(parts, jj)

        loop(8, tables)
        rz_new = scalar_of(tab[3, 0]) + scalar_of(tab[3, 1])
        nxt, prv = halo(ph, following), halo(ph, previous)
        if ph == 0:
            rz = rz_new
            d2[...] = z2[...]
            mvd[...] = mv[...]
        else:
            beta = rz_new / rz
            rz = rz_new
            nxt = nxt + beta * halo(0, following)
            prv = prv + beta * halo(0, previous)
            d2[...] = z2[...] + beta * d2[...]
            mvd[...] = mv[...] + beta * mvd[...]

        def residuals(j):
            v = jnp.where(pos_last, spread(nxt, j + 96), after(d2[rows8(j), :]))
            e2[rows8(j), :] = (v - mvd[rows8(j), :]) * keep_last

        loop(N, residuals)

        for index16, field in ((pf16, near), (ps16, far)):
            index = [index16[pv * 8 : (pv + 1) * 8, :] for pv in range(2)]
            high = [v // 128 for v in index]
            low = [v % 128 for v in index]

            def look(hi, carry):
                carry = list(carry)
                for h in range(2):
                    here = [v == hi * 2 + h for v in high]
                    for j in range(N):
                        src = jnp.broadcast_to(tab[j % 4, h, pl.ds(hi * 4 + j // 4, 1), :], (8, 128))
                        for pv in range(2):
                            k = j * 2 + pv
                            carry[k] = jnp.where(here[pv], jnp.take_along_axis(src, low[pv], axis=1), carry[k])
                return tuple(carry)

            found = lax.fori_loop(0, 16, look, tuple(jnp.zeros((8, 128), F32) for _ in range(30)))
            for j in range(N):
                for pv in range(2):
                    v = found[j * 2 + pv]
                    if ph == 1:
                        v = v + beta * field[j, pv * 8 : (pv + 1) * 8, :]
                    field[j, pv * 8 : (pv + 1) * 8, :] = v

        def forward(i):
            f2[rows16(i), :] = near[i] - jnp.sum(blk[i] * far[...], axis=0)

        loop(N, forward)

        def backward(j):
            b2[rows16(j), :] = -jnp.sum(blk[:, j] * f2[0:240, :].reshape(N, 16, 128), axis=0)

        loop(N, backward)
        own = recv_f[ph, :, rows16(cl), :]
        if ph == 1:
            own = own + beta * recv_f[0, :, rows16(cl), :]
        damped = own * lam[...]
        errors = e2[0:120, :].reshape(N, 8, 128)
        part = total((f2[0:240, :] * f2[0:240, :]).reshape(N, 16, 128)) + total(errors * errors) + total(damped * own)
        fill(f2, 16, 16, 0, 16, oh_p, lhs_p)
        fill(b2, 16, 16, 16, 16, oh_p, lhs_p)
        spread_sum(lhs_p, wt_p, sums, 256)
        row = jnp.where(iota((1, 128), 1) % 32 == 30, part, 0.0)
        messages(sums, 16, row, out_b.at[ph])
        out_b[ph, :, rows16(cl), :] = out_b[ph, :, rows16(cl), :] + damped

        def send_b(t, c):
            pltpu.make_async_remote_copy(
                out_b.at[ph, t % 8, rows4(c * 4 + t // 8), :],
                recv_b.at[ph, tm % 4, cl, rows4(tm // 4), :],
                send_sem.at[ph, 1],
                recv_sem.at[ph, 1],
                device_id=(t, c),
                device_id_type=MESHID,
            ).start()

        sweep(send_b)
        pltpu.make_async_copy(
            out_b.at[ph, tm % 8, rows4(cl * 4 + tm // 8), :], recv_b.at[ph, tm % 4, cl, rows4(tm // 4), :], recv_sem.at[ph, 1]
        ).start()

        errors = e2[0:120, :].reshape(N, 8, 128)

        def inertial(j):
            edge = (d2[rows8(j), :] - spread(prv, j + 96 + N)) * keep_first
            shifted = jnp.where(pos_first, edge, before(e2[rows8(j), :]))
            jv[rows8(j), :] = shifted - jnp.sum(tb[:, j] * errors, axis=0)

        loop(N, inertial)

        pltpu.make_async_copy(recv_b.at[ph], recv_b.at[ph], recv_sem.at[ph, 1]).wait()

        def tables2(gp):
            parts = [jnp.sum(recv_b[ph, gl, :, rows8(gp), :], axis=0) for gl in range(4)]
            for jj in range(4):
                tab2[jj, rows8(gp), :] = regroup(parts, jj)

        loop(4, tables2)
        alpha = rz / scalar_of(tab2[3])
        high, low = slot8[...] // 128, slot8[...] % 128
        for j in range(N):
            v = jv[j * 8 : (j + 1) * 8, :]
            found = jnp.zeros((8, 128), F32)
            for g4 in range(8):
                src = jnp.broadcast_to(tab2[j % 4, g4 * 4 + j // 4 : g4 * 4 + j // 4 + 1, :], (8, 128))
                found = jnp.where(high == g4, jnp.take_along_axis(src, low, axis=1), found)
            at = slice(j * 8, (j + 1) * 8)
            step = alpha * d2[at, :]
            x2[at, :] = step if ph == 0 else x2[at, :] + step
            r2[at, :] = r2[at, :] - alpha * (v + found)

    for a in range(8):
        x_out[:, a * 128 : (a + 1) * 128] = x2[pl.ds(a, 16, stride=8), :][:N, :]
        r_out[:, a * 128 : (a + 1) * 128] = r2[pl.ds(a, 16, stride=8), :][:N, :]
    for ph in range(2):
        for way in range(2):
            sent = sums.at[:, pl.ds(0, 254), :]
            pltpu.make_async_copy(sent, sent, send_sem.at[ph, way]).wait()


def on_device(right_side, transition, precond, slot_of, cluster_id, damping, pair_first, pair_second, pair_blocks):
    vm = pl.BlockSpec(memory_space=pltpu.VMEM)
    anywhere = pl.BlockSpec(memory_space=pl.ANY)
    field = pltpu.VMEM((128, 128), F32)
    call = pl.pallas_call(
        kernel,
        out_shape=(jax.ShapeDtypeStruct((N, 1024), F32),) * 2,
        in_specs=[vm] * 9 + [anywhere] * 3,
        out_specs=(vm, vm),
        scratch_shapes=[
            pltpu.VMEM((N, N, 8, 128), F32),
            pltpu.VMEM((N, N, 8, 128), F32),
            pltpu.VMEM((N, N, 16, 128), F32),
            field, field, field, field, field, field, field, field,
            pltpu.VMEM((N, 16, 128), F32),
            pltpu.VMEM((N, 16, 128), F32),
            pltpu.VMEM((256, 128), F32),
            pltpu.VMEM((256, 128), F32),
            pltpu.VMEM((4, 2, 64, 128), F32),
            pltpu.VMEM((4, 32, 128), F32),
            pltpu.VMEM((2, 256, 128), F32),
            pltpu.VMEM((256, 1024), BF16),
            pltpu.VMEM((64, 1024), BF16),
            pltpu.VMEM((2, 64, 1024), BF16),
            pltpu.VMEM((256, 4096), BF16),
            pltpu.VMEM((256, 4096), BF16),
            pltpu.VMEM((2, 256, 4096), BF16),
            pltpu.VMEM((8, 16, 128), F32),
            pltpu.VMEM((2, 8, 16, 128), F32),
            pltpu.VMEM((2, 8, 64, 128), F32),
            pltpu.VMEM((2, 8, 64, 128), F32),
            pltpu.VMEM((2, 4, 4, 32, 128), F32),
            pltpu.SemaphoreType.DMA((3, 8)),
            pltpu.SemaphoreType.DMA((2, 2)),
            pltpu.SemaphoreType.DMA((2, 2)),
        ],
        compiler_params=pltpu.CompilerParams(collective_id=0, has_side_effects=True, vmem_limit_bytes=60 * 1024 * 1024),
    )
    return call(
        right_side,
        slot_of.reshape(1, 1024),
        slot_of.reshape(8, 128),
        cluster_id.reshape(8, 128),
        jnp.pad(damping, ((0, 0), (0, 64))),
        pair_first.reshape(1, 2048),
        pair_second.reshape(1, 2048),
        pair_first.reshape(16, 128),
        pair_second.reshape(16, 128),
        precond,
        transition,
        pair_blocks.reshape(N, N, 16, 128),
    )


def solution(mesh):
    placed = (
        P(None, ("tm", "clus")),
        P(None, None, ("tm", "clus")),
        P(None, None, ("tm", "clus")),
        P(("tm", "clus")),
        P("tm", "clus"),
        P("tm", None),
        P("tm", "clus"),
        P("tm", "clus"),
        P(None, None, "tm", "clus"),
    )
    return jax.shard_map(
        on_device,
        mesh=mesh,
        in_specs=placed,
        out_specs=(P(None, ("tm", "clus")), P(None, ("tm", "clus"))),
        check_vma=False,
    )
```

```python
import jax
import jax.numpy as jnp
from jax import lax
from jax.experimental import pallas as pl
from jax.experimental.pallas import tpu as pltpu
from jax.sharding import PartitionSpec as P

MESHID = pl.DeviceIdType.MESH
F32 = jnp.float32
BF16 = jnp.bfloat16
N = 15


def hops(d):
    return min(d, 4 - d)


OFFSETS = sorted(
    ((z, y, c, x) for z in range(4) for y in range(4) for c in range(2) for x in range(4) if z or y or c or x),
    key=lambda o: -hops(o[0]) - hops(o[1]) - hops(o[3]),
)


def place():
    tm = lax.axis_index("tm")
    return lax.div(tm, 8), lax.rem(lax.div(tm, 2), 4), lax.rem(tm, 2), lax.axis_index("clus")


def sweep(action):
    sizes = (4, 4, 2, 4)
    turned = [[lax.rem(at + d, n) for d in range(n)] for at, n in zip(place(), sizes)]
    for offset in OFFSETS:
        action(*(turned[k][d] for k, d in enumerate(offset)))


def device(z, y, core, x):
    return (z * 8 + y * 2 + core, x)


def iota(shape, axis):
    return lax.broadcasted_iota(jnp.int32, shape, axis)


def total(v):
    while v.ndim > 2:
        v = jnp.sum(v, axis=0)
    return jnp.sum(v, axis=(0, 1), keepdims=True)


def loop(n, body, unroll=1):
    def step(i, c):
        body(i)
        return c

    lax.fori_loop(0, n, step, 0, unroll=unroll)


def rows8(i):
    return pl.ds(pl.multiple_of(i * 8, 8), 8)


def rows16(i):
    return pl.ds(pl.multiple_of(i * 16, 16), 16)


def rows4(i):
    return pl.ds(pl.multiple_of(i * 4, 4), 4)


def lanes(i):
    return pl.ds(pl.multiple_of(i * 128, 128), 128)


def multiply(blocks, src, dst):
    field = src[0:N]

    def one(i):
        dst[rows8(i), :] = jnp.sum(blocks[i] * field, axis=0)

    loop(N, one)


def after(v):
    turned = pltpu.roll(v, 127, axis=1)
    return jnp.where(iota((8, 128), 1) == 127, pltpu.roll(turned, 7, axis=0), turned)


def before(v):
    turned = pltpu.roll(v, 1, axis=1)
    return jnp.where(iota((8, 128), 1) == 0, pltpu.roll(turned, 1, axis=0), turned)


def spread(row, j):
    return jnp.take_along_axis(jnp.broadcast_to(row, (8, 128)), jnp.full((8, 128), j, jnp.int32), axis=1)


def extras(z2, mv2, scalar):
    lane, sub = iota((16, 128), 1), iota((16, 128), 0)
    first = jnp.sum(jnp.where(lane == 0, z2[pl.ds(0, 16, stride=8), :], 0.0), axis=1, keepdims=True)
    last = jnp.sum(jnp.where(lane == 127, mv2[pl.ds(7, 16, stride=8), :], 0.0), axis=1, keepdims=True)
    row = jnp.where(lane % 32 == sub, first, 0.0) + jnp.where(lane % 32 == sub + N, last, 0.0)
    return jnp.where(iota((1, 128), 1) % 32 == 30, scalar, jnp.sum(row, axis=0, keepdims=True))


def fill(src2, stride, tiles, base, count, onehot, lhs):
    def one(a):
        v = src2[pl.ds(a, 16, stride=stride), :]
        high = v.astype(BF16)
        low = (v - high.astype(F32)).astype(BF16)
        cols = lanes(base + a)
        for n in range(count):
            mask = onehot[n * 16 : (n + 1) * 16, cols]
            lhs[n * 16 : (n + 1) * 16, cols] = high * mask
            lhs[(count + n) * 16 : (count + n + 1) * 16, cols] = low * mask

    loop(tiles, one, 2)


def spread_sum(lhs, wt, sums, count):
    made = lax.dot_general(lhs[...], wt[...], (((1,), (1,)), ((), ())), preferred_element_type=F32)
    made = made[0:count] + made[count:]
    sums[0, 0:count, :] = made[:, 0:128]
    sums[1, 0:count, :] = made[:, 128:256]


def messages(sums, count, row, out):
    for half in range(2):
        sums[half, pl.ds(N, count, stride=16), :] = jnp.broadcast_to(row, (count, 128))
    group = iota((8, 128), 1) // 32

    def one(hp):
        for half in range(2):
            made = [None] * 4
            for jj in range(4):
                v = sums[half, pl.ds(hp * 32 + jj, 8, stride=4), :]
                for tl in range(4):
                    turn = ((jj - tl) % 4) * 32
                    moved = pltpu.roll(v, turn, axis=1) if turn else v
                    made[tl] = moved if jj == 0 else jnp.where(group == jj, moved, made[tl])
            for tl in range(4):
                out[half * 4 + tl, rows8(hp), :] = made[tl]

    loop(count // 2, one, 2)


def regroup(parts, jj):
    group = iota((8, 128), 1) // 32
    made = None
    for tl in range(4):
        turn = ((tl - jj) % 4) * 32
        moved = pltpu.roll(parts[tl], turn, axis=1) if turn else parts[tl]
        made = moved if tl == 0 else jnp.where(group == tl, moved, made)
    return made


def scalar_of(v):
    keep = (iota(v.shape, 0) % 4 == 3) & (iota(v.shape, 1) % 32 == 30)
    return total(jnp.where(keep, v, 0.0))


def kernel(
    b_any, slot_any, slot8_any, cid8_any, damp_any, pf_any, ps_any, pf16_any, ps16_any, m_any, t_any, blk_any,
    out,
    slot_row, slot8, cid8, damp, pf_row, ps_row, pf16, ps16,
    mb, tb, blk, r3, z2, d2, mv, ez, e2, jv, near, far, f2, b2, tab, tab2, sums,
    wt_s, oh_s, lhs_s, wt_p, oh_p, lhs_p, lam, out_f, out_b, recv_f, recv_b,
    load_sem, send_sem, recv_sem,
):
    tm = lax.axis_index("tm")
    cl = lax.axis_index("clus")
    flat = tm * 4 + cl
    my_z, my_y, my_core, my_x = place()
    my_tl = my_y * 2 + my_core
    bar = pltpu.get_barrier_semaphore()
    sweep(lambda *who: pl.semaphore_signal(bar, 1, device_id=device(*who), device_id_type=MESHID))

    def spread_load(n, src, dst):
        if len(dst.shape) == 3:
            return [
                pltpu.make_async_copy(src.at[:, pl.ds(a * 128, 128)], dst.at[pl.ds(0, N), a, :], load_sem.at[n, a]) for a in range(8)
            ]
        return [pltpu.make_async_copy(src.at[:, :, pl.ds(a * 128, 128)], dst.at[:, :, a, :], load_sem.at[n, a]) for a in range(8)]

    small = ((slot_any, slot_row), (slot8_any, slot8), (cid8_any, cid8), (damp_any, damp))
    small += ((pf_any, pf_row), (ps_any, ps_row), (pf16_any, pf16), (ps16_any, ps16))
    load_small = [pltpu.make_async_copy(src, dst, load_sem.at[3, n]) for n, (src, dst) in enumerate(small)]
    load_r, load_m, load_t = spread_load(0, b_any, r3), spread_load(1, m_any, mb), spread_load(2, t_any, tb)
    load_blk = pltpu.make_async_copy(blk_any, blk, load_sem.at[4, 0])
    for copy in load_small[:1] + load_r + load_m + load_t + load_small[1:]:
        copy.start()

    z2[120:128, :] = jnp.zeros((8, 128), F32)
    mv[120:128, :] = jnp.zeros((8, 128), F32)
    f2[240:256, :] = jnp.zeros((16, 128), F32)
    b2[240:256, :] = jnp.zeros((16, 128), F32)
    load_small[0].wait()

    def slots(a):
        index = slot_row[:, lanes(a)]
        wt_s[:, lanes(a)] = jnp.where(iota((256, 128), 0) == index % 256, 1.0, 0.0).astype(BF16)
        oh_s[:, lanes(a)] = jnp.where(iota((64, 128), 0) // 16 == index // 256, 1.0, 0.0).astype(BF16)

    loop(8, slots, 2)
    for copy in load_r:
        copy.wait()

    pos_first = (iota((8, 128), 0) == 0) & (iota((8, 128), 1) == 0)
    pos_last = (iota((8, 128), 0) == 7) & (iota((8, 128), 1) == 127)
    keep_last = jnp.where(pos_last & (flat == 127), 0.0, 1.0)
    keep_first = jnp.where(pos_first & (flat == 0), 0.0, 1.0)
    following, previous = (flat + 1) % 128, (flat + 127) % 128

    def halo(ph, who):
        return recv_f[ph, (who // 4) % 8, pl.ds(((who % 4) * 4 + who // 32) * 4 + 3, 1), :]

    rz = None
    for ph in range(2):
        if ph == 0:
            for copy in load_m:
                copy.wait()
            load_blk.start()
        multiply(mb, r3, z2)
        z3 = z2[0:120, :].reshape(N, 8, 128)
        part = total(r3[0:N] * z3)
        if ph == 0:
            for copy in load_t:
                copy.wait()
        multiply(tb, z3, mv)
        row = extras(z2, mv, part)
        fill(z2, 8, 8, 0, 4, oh_s, lhs_s)
        spread_sum(lhs_s, wt_s, sums, 64)
        messages(sums, 4, row, out_f.at[ph])
        if ph == 0:
            pl.semaphore_wait(bar, 127)

        def send_f(z, y, core, x):
            pltpu.make_async_remote_copy(
                out_f.at[ph, y * 2 + core, rows4(z), :],
                recv_f.at[ph, my_tl, rows4(my_x * 4 + my_z), :],
                send_sem.at[ph, 0],
                recv_sem.at[ph, 0],
                device_id=device(z, y, core, x),
                device_id_type=MESHID,
            ).start()

        sweep(send_f)
        pltpu.make_async_copy(
            out_f.at[ph, my_tl, rows4(my_z), :], recv_f.at[ph, my_tl, rows4(my_x * 4 + my_z), :], recv_sem.at[ph, 0]
        ).start()

        for j in range(N):
            at = slice(j * 8, (j + 1) * 8)
            ez[at, :] = jnp.where(pos_last, 0.0, after(z2[at, :])) - mv[at, :]
        if ph == 0:
            for copy in load_small[1:]:
                copy.wait()

            def pairs(a):
                for base, ref in ((0, pf_row), (16, ps_row)):
                    index = ref[:, lanes(a)]
                    wt_p[:, lanes(base + a)] = jnp.where(iota((256, 128), 0) == index % 256, 1.0, 0.0).astype(BF16)
                    oh_p[:, lanes(base + a)] = jnp.where(iota((256, 128), 0) // 16 == index // 256, 1.0, 0.0).astype(BF16)

            loop(16, pairs, 2)
            per = jnp.take_along_axis(jnp.broadcast_to(jnp.concatenate([damp[...]] * 2, axis=1), (8, 128)), cid8[...], axis=1)
            group = iota((8, 128), 1) // 32
            spare = (iota((4, 128), 0) == 3) & (iota((4, 128), 1) >= 96)
            for tl in range(4):
                wide = None
                for jj in range(4):
                    turn = ((jj - tl) % 4) * 32
                    moved = pltpu.roll(per, turn, axis=1) if turn else per
                    wide = moved if jj == 0 else jnp.where(group == jj, moved, wide)
                for t4 in range(8):
                    th, h = t4 // 2, t4 % 2
                    lam[h * 4 + tl, th * 4 : (th + 1) * 4, :] = jnp.where(spare, 0.0, jnp.broadcast_to(wide[t4 : t4 + 1, :], (4, 128)))
            load_blk.wait()

        pltpu.make_async_copy(recv_f.at[ph], recv_f.at[ph], recv_sem.at[ph, 0]).wait()

        def tables(hp):
            for h in range(2):
                parts = [recv_f[ph, h * 4 + tl, rows8(hp), :] for tl in range(4)]
                for jj in range(4):
                    tab[jj, h, rows8(hp), :] = regroup(parts, jj)

        loop(8, tables, 2)
        rz_new = scalar_of(tab[3, 0]) + scalar_of(tab[3, 1])
        nxt, prv = halo(ph, following), halo(ph, previous)
        if ph == 0:
            rz = rz_new
            d2[...] = z2[...]
        else:
            beta = rz_new / rz
            rz = rz_new
            prv = prv + beta * halo(0, previous)
            d2[...] = z2[...] + beta * d2[...]
        part = jnp.zeros((8, 128), F32)
        for j in range(N):
            at = slice(j * 8, (j + 1) * 8)
            v = (ez[at, :] + jnp.where(pos_last, spread(nxt, j + 96), 0.0)) * keep_last
            if ph == 1:
                v = v + beta * e2[at, :]
            e2[at, :] = v
            part = part + v * v
        part = total(part)

        for index16, field in ((pf16, near), (ps16, far)):
            index = [index16[pv * 8 : (pv + 1) * 8, :] for pv in range(2)]
            high = [v // 128 for v in index]
            low = [v % 128 for v in index]

            def look(quad, carry):
                carry = list(carry)
                for low_hi in range(4):
                    for h in range(2):
                        here = [v == quad * 8 + low_hi * 2 + h for v in high]
                        for j in range(N):
                            row = tab[j % 4, h, pl.ds(quad * 16 + low_hi * 4 + j // 4, 1), :]
                            src = jnp.broadcast_to(row, (8, 128))
                            for pv in range(2):
                                k = j * 2 + pv
                                carry[k] = jnp.where(here[pv], jnp.take_along_axis(src, low[pv], axis=1), carry[k])
                return tuple(carry)

            found = lax.fori_loop(0, 4, look, tuple(jnp.zeros((8, 128), F32) for _ in range(30)))
            for j in range(N):
                for pv in range(2):
                    v = found[j * 2 + pv]
                    if ph == 1:
                        v = v + beta * field[j, pv * 8 : (pv + 1) * 8, :]
                    field[j, pv * 8 : (pv + 1) * 8, :] = v

        def forward(i):
            f2[rows16(i), :] = near[i] - jnp.sum(blk[i] * far[...], axis=0)

        loop(N, forward, 3)

        def backward(j):
            b2[rows16(j), :] = -jnp.sum(blk[:, j] * f2[0:240, :].reshape(N, 16, 128), axis=0)

        loop(N, backward, 3)
        own = recv_f[ph, :, rows16(cl), :]
        if ph == 1:
            own = own + beta * recv_f[0, :, rows16(cl), :]
        damped = own * lam[...]
        part = part + total((f2[0:240, :] * f2[0:240, :]).reshape(N, 16, 128)) + total(damped * own)
        fill(f2, 16, 16, 0, 16, oh_p, lhs_p)
        fill(b2, 16, 16, 16, 16, oh_p, lhs_p)
        spread_sum(lhs_p, wt_p, sums, 256)
        row = jnp.where(iota((1, 128), 1) % 32 == 30, part, 0.0)
        messages(sums, 16, row, out_b.at[ph])
        out_b[ph, :, rows16(cl), :] = out_b[ph, :, rows16(cl), :] + damped

        def send_b(z, y, core, x):
            pltpu.make_async_remote_copy(
                out_b.at[ph, y * 2 + core, rows4(x * 4 + z), :],
                recv_b.at[ph, lax.rem(my_tl, 4), my_x, rows4(my_z * 2 + lax.div(my_tl, 4)), :],
                send_sem.at[ph, 1],
                recv_sem.at[ph, 1],
                device_id=device(z, y, core, x),
                device_id_type=MESHID,
            ).start()

        sweep(send_b)
        pltpu.make_async_copy(
            out_b.at[ph, my_tl, rows4(my_x * 4 + my_z), :],
            recv_b.at[ph, lax.rem(my_tl, 4), my_x, rows4(my_z * 2 + lax.div(my_tl, 4)), :],
            recv_sem.at[ph, 1],
        ).start()

        errors = e2[0:120, :].reshape(N, 8, 128)

        def inertial(j):
            edge = (d2[rows8(j), :] - spread(prv, j + 96 + N)) * keep_first
            shifted = jnp.where(pos_first, edge, before(e2[rows8(j), :]))
            jv[rows8(j), :] = shifted - jnp.sum(tb[:, j] * errors, axis=0)

        loop(N, inertial, 3)

        pltpu.make_async_copy(recv_b.at[ph], recv_b.at[ph], recv_sem.at[ph, 1]).wait()

        def tables2(gp):
            parts = [jnp.sum(recv_b[ph, gl, :, rows8(gp), :], axis=0) for gl in range(4)]
            for jj in range(4):
                tab2[jj, rows8(gp), :] = regroup(parts, jj)

        loop(4, tables2, 4)
        alpha = rz / scalar_of(tab2[3])
        high, low = slot8[...] // 128, slot8[...] % 128
        for j in range(N):
            v = jv[j * 8 : (j + 1) * 8, :]
            found = jnp.zeros((8, 128), F32)
            for g4 in range(8):
                src = jnp.broadcast_to(tab2[j % 4, g4 * 4 + j // 4 : g4 * 4 + j // 4 + 1, :], (8, 128))
                found = jnp.where(high == g4, jnp.take_along_axis(src, low, axis=1), found)
            at = slice(j * 8, (j + 1) * 8)
            step = alpha * d2[at, :]
            out[0, j] = step if ph == 0 else out[0, j] + step
            r3[j] = r3[j] - alpha * (v + found)

    out[1] = r3[...]
    for ph in range(2):
        for way in range(2):
            sent = sums.at[:, pl.ds(0, 254), :]
            pltpu.make_async_copy(sent, sent, send_sem.at[ph, way]).wait()


def finish(both, x_out, r_out, sem):
    copies = [
        pltpu.make_async_copy(both.at[n, pl.ds(0, N), a, :], dst.at[:, pl.ds(a * 128, 128)], sem.at[n, a])
        for n, dst in enumerate((x_out, r_out))
        for a in range(8)
    ]
    for copy in copies:
        copy.start()
    for copy in copies:
        copy.wait()


def on_device(right_side, transition, precond, slot_of, cluster_id, damping, pair_first, pair_second, pair_blocks):
    vm = pl.BlockSpec(memory_space=pltpu.VMEM)
    anywhere = pl.BlockSpec(memory_space=pl.ANY)
    field = pltpu.VMEM((128, 128), F32)
    whole = jnp.int32
    both = pl.pallas_call(
        kernel,
        out_shape=jax.ShapeDtypeStruct((2, 16, 8, 128), F32),
        in_specs=[anywhere] * 12,
        out_specs=vm,
        scratch_shapes=[
            pltpu.VMEM((1, 1024), whole), pltpu.VMEM((8, 128), whole), pltpu.VMEM((8, 128), whole), pltpu.VMEM((1, 64), F32),
            pltpu.VMEM((1, 2048), whole), pltpu.VMEM((1, 2048), whole), pltpu.VMEM((16, 128), whole), pltpu.VMEM((16, 128), whole),
            pltpu.VMEM((N, N, 8, 128), F32),
            pltpu.VMEM((N, N, 8, 128), F32),
            pltpu.VMEM((N, N, 16, 128), F32),
            pltpu.VMEM((16, 8, 128), F32),
            field, field, field, field, field, field,
            pltpu.VMEM((N, 16, 128), F32),
            pltpu.VMEM((N, 16, 128), F32),
            pltpu.VMEM((256, 128), F32),
            pltpu.VMEM((256, 128), F32),
            pltpu.VMEM((4, 2, 64, 128), F32),
            pltpu.VMEM((4, 32, 128), F32),
            pltpu.VMEM((2, 256, 128), F32),
            pltpu.VMEM((256, 1024), BF16),
            pltpu.VMEM((64, 1024), BF16),
            pltpu.VMEM((128, 1024), BF16),
            pltpu.VMEM((256, 4096), BF16),
            pltpu.VMEM((256, 4096), BF16),
            pltpu.VMEM((512, 4096), BF16),
            pltpu.VMEM((8, 16, 128), F32),
            pltpu.VMEM((2, 8, 16, 128), F32),
            pltpu.VMEM((2, 8, 64, 128), F32),
            pltpu.VMEM((2, 8, 64, 128), F32),
            pltpu.VMEM((2, 4, 4, 32, 128), F32),
            pltpu.SemaphoreType.DMA((5, 8)),
            pltpu.SemaphoreType.DMA((2, 2)),
            pltpu.SemaphoreType.DMA((2, 2)),
        ],
        compiler_params=pltpu.CompilerParams(collective_id=0, has_side_effects=True, vmem_limit_bytes=60 * 1024 * 1024),
    )(
        right_side,
        slot_of.reshape(1, 1024),
        slot_of.reshape(8, 128),
        cluster_id.reshape(8, 128),
        damping,
        pair_first.reshape(1, 2048),
        pair_second.reshape(1, 2048),
        pair_first.reshape(16, 128),
        pair_second.reshape(16, 128),
        precond,
        transition,
        pair_blocks.reshape(N, N, 16, 128),
    )
    return pl.pallas_call(
        finish,
        out_shape=(jax.ShapeDtypeStruct((N, 1024), F32),) * 2,
        in_specs=[vm],
        out_specs=(anywhere, anywhere),
        scratch_shapes=[pltpu.SemaphoreType.DMA((2, 8))],
    )(both)


def solution(mesh):
    placed = (
        P(None, ("tm", "clus")),
        P(None, None, ("tm", "clus")),
        P(None, None, ("tm", "clus")),
        P(("tm", "clus")),
        P("tm", "clus"),
        P("tm", None),
        P("tm", "clus"),
        P("tm", "clus"),
        P(None, None, "tm", "clus"),
    )
    return jax.shard_map(
        on_device,
        mesh=mesh,
        in_specs=placed,
        out_specs=(P(None, ("tm", "clus")), P(None, ("tm", "clus"))),
        check_vma=False,
    )
```

```python
import jax
import jax.numpy as jnp
from jax import lax
from jax.experimental import pallas as pl
from jax.experimental.pallas import tpu as pltpu
from jax.sharding import PartitionSpec as P

MESHID = pl.DeviceIdType.MESH
F32 = jnp.float32
BF16 = jnp.bfloat16
N = 15


def hops(d):
    return min(d, 4 - d)


OFFSETS = sorted(
    ((z, y, c, x) for z in range(4) for y in range(4) for c in range(2) for x in range(4) if z or y or c or x),
    key=lambda o: -hops(o[0]) - hops(o[1]) - hops(o[3]),
)


TURNS = ((2, 1, 3, 0),)


def place():
    tm = lax.axis_index("tm")
    return lax.div(tm, 8), lax.rem(lax.div(tm, 2), 4), lax.rem(tm, 2), lax.axis_index("clus")


def sweep(action, turns=(0, 1, 2, 3)):
    sizes = (4, 4, 2, 4)
    turned = [[lax.rem(at + d, n) for d in range(n)] for at, n in zip(place(), sizes)]
    for offset in OFFSETS:
        if offset[3] in turns:
            action(*(turned[k][d] for k, d in enumerate(offset)))


def device(z, y, core, x):
    return (z * 8 + y * 2 + core, x)


def iota(shape, axis):
    return lax.broadcasted_iota(jnp.int32, shape, axis)


def total(v):
    while v.ndim > 2:
        v = jnp.sum(v, axis=0)
    return jnp.sum(v, axis=(0, 1), keepdims=True)


def loop(n, body, unroll=1):
    def step(i, c):
        body(i)
        return c

    lax.fori_loop(0, n, step, 0, unroll=unroll)


def rows8(i):
    return pl.ds(pl.multiple_of(i * 8, 8), 8)


def rows16(i):
    return pl.ds(pl.multiple_of(i * 16, 16), 16)


def rows4(i):
    return pl.ds(pl.multiple_of(i * 4, 4), 4)


def lanes(i):
    return pl.ds(pl.multiple_of(i * 128, 128), 128)


def multiply(blocks, src, dst):
    field = src[0:N]

    def one(i):
        dst[rows8(i), :] = jnp.sum(blocks[i] * field, axis=0)

    loop(N, one, N)


def after(v):
    turned = pltpu.roll(v, 127, axis=1)
    return jnp.where(iota((8, 128), 1) == 127, pltpu.roll(turned, 7, axis=0), turned)


def before(v):
    turned = pltpu.roll(v, 1, axis=1)
    return jnp.where(iota((8, 128), 1) == 0, pltpu.roll(turned, 1, axis=0), turned)


def spread(row, j):
    return jnp.take_along_axis(jnp.broadcast_to(row, (8, 128)), jnp.full((8, 128), j, jnp.int32), axis=1)


def extras(z2, mv2, scalar):
    lane, sub = iota((16, 128), 1), iota((16, 128), 0)
    first = jnp.sum(jnp.where(lane == 0, z2[pl.ds(0, 16, stride=8), :], 0.0), axis=1, keepdims=True)
    last = jnp.sum(jnp.where(lane == 127, mv2[pl.ds(7, 16, stride=8), :], 0.0), axis=1, keepdims=True)
    row = jnp.where(lane % 32 == sub, first, 0.0) + jnp.where(lane % 32 == sub + N, last, 0.0)
    return jnp.where(iota((1, 128), 1) % 32 == 30, scalar, jnp.sum(row, axis=0, keepdims=True))


def fill(src2, stride, tiles, base, count, onehot, lhs):
    def one(a):
        v = src2[pl.ds(a, 16, stride=stride), :]
        high = v.astype(BF16)
        low = (v - high.astype(F32)).astype(BF16)
        cols = lanes(base + a)
        for n in range(count):
            mask = onehot[n * 16 : (n + 1) * 16, cols]
            lhs[n * 16 : (n + 1) * 16, cols] = high * mask
            lhs[(count + n) * 16 : (count + n + 1) * 16, cols] = low * mask

    loop(tiles, one, 2)


def spread_sum(lhs, wt, sums, base, count):
    made = lax.dot_general(lhs, wt[...], (((1,), (1,)), ((), ())), preferred_element_type=F32)
    made = made[0:count] + made[count:]
    sums[0, base : base + count, :] = made[:, 0:128]
    sums[1, base : base + count, :] = made[:, 128:256]


def messages(sums, base, count, row, store):
    for half in range(2):
        sums[half, pl.ds(base + N, count, stride=16), :] = jnp.broadcast_to(row, (count, 128))
    for hp in range(count // 2):
        for half in range(2):
            made = regroup([sums[half, pl.ds(base + hp * 32 + jj, 8, stride=4), :] for jj in range(4)])
            for tl in range(4):
                store(half * 4 + tl, hp, made[tl])


def regroup(v):
    group = iota((8, 128), 1) // 32
    low, even = group < 2, group % 2 == 0
    a = [jnp.where(low, v[i], pltpu.roll(v[i + 2], 64, axis=1)) for i in range(2)]
    a += [jnp.where(low, pltpu.roll(v[i], 64, axis=1), v[i + 2]) for i in range(2)]
    out = []
    for i in (0, 2):
        out.append(jnp.where(even, a[i], pltpu.roll(a[i + 1], 32, axis=1)))
        out.append(jnp.where(even, pltpu.roll(a[i], 96, axis=1), a[i + 1]))
    return out


def scalar_of(v):
    keep = (iota(v.shape, 0) % 4 == 3) & (iota(v.shape, 1) % 32 == 30)
    return total(jnp.where(keep, v, 0.0))


def kernel(
    b_any, slot_any, slot8_any, cid8_any, damp_any, pf_any, ps_any, pf16_any, ps16_any, m_any, t_any, blk_any,
    out,
    slot_row, slot8, cid8, damp, pf_row, ps_row, pf16, ps16,
    mb, tb, blk, r3, z2, d2, mv, ez, e2, jv, near, far, f2, b2, tab, tab2, sums,
    wt_s, oh_s, lhs_s, wt_p, oh_p, parts_p, lhs_p, lam, out_f, out_b, recv_f, recv_b,
    load_sem, send_sem, recv_sem,
):
    tm = lax.axis_index("tm")
    cl = lax.axis_index("clus")
    flat = tm * 4 + cl
    my_z, my_y, my_core, my_x = place()
    my_tl = my_y * 2 + my_core
    bar = pltpu.get_barrier_semaphore()
    sweep(lambda *who: pl.semaphore_signal(bar, 1, device_id=device(*who), device_id_type=MESHID))

    def spread_load(n, src, dst):
        if len(dst.shape) == 3:
            return [
                pltpu.make_async_copy(src.at[:, pl.ds(a * 128, 128)], dst.at[pl.ds(0, N), a, :], load_sem.at[n, a]) for a in range(8)
            ]
        return [pltpu.make_async_copy(src.at[:, :, pl.ds(a * 128, 128)], dst.at[:, :, a, :], load_sem.at[n, a]) for a in range(8)]

    small = ((slot_any, slot_row), (slot8_any, slot8), (cid8_any, cid8), (damp_any, damp))
    small += ((pf_any, pf_row), (ps_any, ps_row), (pf16_any, pf16), (ps16_any, ps16))
    load_small = [pltpu.make_async_copy(src, dst, load_sem.at[3, n]) for n, (src, dst) in enumerate(small)]
    load_r, load_m, load_t = spread_load(0, b_any, r3), spread_load(1, m_any, mb), spread_load(2, t_any, tb)
    load_blk = pltpu.make_async_copy(blk_any, blk, load_sem.at[4, 0])
    for copy in load_small[:1] + load_r + load_m + load_t + load_small[1:]:
        copy.start()

    z2[120:128, :] = jnp.zeros((8, 128), F32)
    mv[120:128, :] = jnp.zeros((8, 128), F32)
    f2[240:256, :] = jnp.zeros((16, 128), F32)
    b2[240:256, :] = jnp.zeros((16, 128), F32)
    load_small[0].wait()

    def slots(a):
        index = slot_row[:, lanes(a)]
        wt_s[:, lanes(a)] = jnp.where(iota((256, 128), 0) == index % 256, 1.0, 0.0).astype(BF16)
        oh_s[:, lanes(a)] = jnp.where(iota((64, 128), 0) // 16 == index // 256, 1.0, 0.0).astype(BF16)

    loop(8, slots, 2)
    for copy in load_r:
        copy.wait()

    pos_first = (iota((8, 128), 0) == 0) & (iota((8, 128), 1) == 0)
    pos_last = (iota((8, 128), 0) == 7) & (iota((8, 128), 1) == 127)
    keep_last = jnp.where(pos_last & (flat == 127), 0.0, 1.0)
    keep_first = jnp.where(pos_first & (flat == 0), 0.0, 1.0)
    following, previous = (flat + 1) % 128, (flat + 127) % 128

    def halo(ph, who):
        return recv_f[ph, (who // 4) % 8, pl.ds(((who % 4) * 4 + who // 32) * 4 + 3, 1), :]

    out[...] = jnp.zeros_like(out)
    for field in (d2, e2, near, far):
        field[...] = jnp.zeros_like(field)

    def phase(ph, rz):
        @pl.when(ph == 0)
        def _():
            for copy in load_m:
                copy.wait()
            load_blk.start()

        multiply(mb, r3, z2)
        z3 = z2[0:120, :].reshape(N, 8, 128)
        part = total(r3[0:N] * z3)

        @pl.when(ph == 0)
        def _():
            for copy in load_t:
                copy.wait()

        multiply(tb, z3, mv)
        row = extras(z2, mv, part)
        fill(z2, 8, 8, 0, 4, oh_s, lhs_s)
        spread_sum(lhs_s[...], wt_s, sums, 0, 64)

        def keep_f(tl, hp, v):
            out_f[ph, tl, hp * 8 : (hp + 1) * 8, :] = v

        messages(sums, 0, 4, row, keep_f)

        @pl.when(ph == 0)
        def _():
            pl.semaphore_wait(bar, 127)

        def send_f(z, y, core, x):
            pltpu.make_async_remote_copy(
                out_f.at[ph, y * 2 + core, rows4(z), :],
                recv_f.at[ph, my_tl, rows4(my_x * 4 + my_z), :],
                send_sem.at[ph, 0],
                recv_sem.at[ph, my_x],
                device_id=device(z, y, core, x),
                device_id_type=MESHID,
            ).start()

        sweep(send_f)
        pltpu.make_async_copy(
            out_f.at[ph, my_tl, rows4(my_z), :], recv_f.at[ph, my_tl, rows4(my_x * 4 + my_z), :], recv_sem.at[ph, my_x]
        ).start()

        for j in range(N):
            at = slice(j * 8, (j + 1) * 8)
            ez[at, :] = jnp.where(pos_last, 0.0, after(z2[at, :])) - mv[at, :]
        @pl.when(ph == 0)
        def _():
            for copy in load_small[1:]:
                copy.wait()

            def pairs(a):
                for base, ref in ((0, pf_row), (16, ps_row)):
                    index = ref[:, lanes(a)]
                    wt_p[:, lanes(base + a)] = jnp.where(iota((256, 128), 0) == index % 256, 1.0, 0.0).astype(BF16)
                    oh_p[:, lanes(base + a)] = jnp.where(iota((256, 128), 0) // 16 == index // 256, 1.0, 0.0).astype(BF16)

            loop(16, pairs, 2)
            per = jnp.take_along_axis(jnp.broadcast_to(jnp.concatenate([damp[...]] * 2, axis=1), (8, 128)), cid8[...], axis=1)
            group = iota((8, 128), 1) // 32
            spare = (iota((4, 128), 0) == 3) & (iota((4, 128), 1) >= 96)
            for tl in range(4):
                wide = None
                for jj in range(4):
                    turn = ((jj - tl) % 4) * 32
                    moved = pltpu.roll(per, turn, axis=1) if turn else per
                    wide = moved if jj == 0 else jnp.where(group == jj, moved, wide)
                for t4 in range(8):
                    th, h = t4 // 2, t4 % 2
                    lam[h * 4 + tl, th * 4 : (th + 1) * 4, :] = jnp.where(spare, 0.0, jnp.broadcast_to(wide[t4 : t4 + 1, :], (4, 128)))
            load_blk.wait()

        for c in range(4):
            block = recv_f.at[ph, :, c * 16 : (c + 1) * 16, :]
            pltpu.make_async_copy(block, block, recv_sem.at[ph, c]).wait()

        def tables(hp):
            for h in range(2):
                parts = regroup([recv_f[ph, h * 4 + tl, rows8(hp), :] for tl in range(4)])
                for jj in range(4):
                    tab[jj, h, rows8(hp), :] = parts[jj]

        loop(8, tables, 8)
        rz_new = scalar_of(tab[3, 0]) + scalar_of(tab[3, 1])
        beta = jnp.where(ph == 0, 0.0, rz_new / rz)
        rz = rz_new
        nxt = halo(ph, following)
        prv = halo(ph, previous) + beta * halo(0, previous)
        d2[...] = z2[...] + beta * d2[...]
        part = jnp.zeros((8, 128), F32)
        for j in range(N):
            at = slice(j * 8, (j + 1) * 8)
            v = (ez[at, :] + jnp.where(pos_last, spread(nxt, j + 96), 0.0)) * keep_last
            v = v + beta * e2[at, :]
            e2[at, :] = v
            part = part + v * v
        part = total(part)

        for index16, field in ((pf16, near), (ps16, far)):
            index = [index16[pv * 8 : (pv + 1) * 8, :] for pv in range(2)]
            high = [v // 128 for v in index]
            low = [v % 128 for v in index]

            def look(quad, carry):
                carry = list(carry)
                for low_hi in range(4):
                    for h in range(2):
                        here = [v == quad * 8 + low_hi * 2 + h for v in high]
                        for j in range(N):
                            row = tab[j % 4, h, pl.ds(quad * 16 + low_hi * 4 + j // 4, 1), :]
                            src = jnp.broadcast_to(row, (8, 128))
                            for pv in range(2):
                                k = j * 2 + pv
                                carry[k] = jnp.where(here[pv], jnp.take_along_axis(src, low[pv], axis=1), carry[k])
                return tuple(carry)

            found = lax.fori_loop(0, 4, look, tuple(jnp.zeros((8, 128), F32) for _ in range(30)))
            for j in range(N):
                for pv in range(2):
                    v = found[j * 2 + pv]
                    v = v + beta * field[j, pv * 8 : (pv + 1) * 8, :]
                    field[j, pv * 8 : (pv + 1) * 8, :] = v

        def forward(i):
            f2[rows16(i), :] = near[i] - jnp.sum(blk[i] * far[...], axis=0)

        loop(N, forward, 3)

        def backward(j):
            b2[rows16(j), :] = -jnp.sum(blk[:, j] * f2[0:240, :].reshape(N, 16, 128), axis=0)

        loop(N, backward, 3)
        own = recv_f[ph, :, rows16(cl), :] + beta * recv_f[0, :, rows16(cl), :]
        damped = own * lam[...]
        part = part + total((f2[0:240, :] * f2[0:240, :]).reshape(N, 16, 128)) + total(damped * own)
        row = jnp.where(iota((1, 128), 1) % 32 == 30, part, 0.0)
        for base, src in ((0, f2), (16, b2)):
            for a in range(16):
                v = src[pl.ds(a, 16, stride=16), :]
                high = v.astype(BF16)
                cols = slice((base + a) * 128, (base + a + 1) * 128)
                parts_p[0, :, cols] = high
                parts_p[1, :, cols] = (v - high.astype(F32)).astype(BF16)

        def fill_for(k, group):
            for a in range(32):
                cols = slice(a * 128, (a + 1) * 128)
                both = [parts_p[n, :, cols] for n in range(2)]
                for i, c in enumerate(group):
                    for n in range(4):
                        mask = oh_p[rows16(c * 4 + n), cols]
                        for m in range(2):
                            at = ((k * 2 + m) * len(group) + i) * 64 + n * 16
                            lhs_p[at : at + 16, cols] = both[m] * mask

        turns = TURNS
        xs = [[lax.rem(my_x + turn, 4) for turn in group] for group in turns]
        wide = len(turns[0]) * 64
        fill_for(0, xs[0])
        for k, group in enumerate(turns):
            if k + 1 < len(turns):
                fill_for(k + 1, xs[k + 1])
            spread_sum(lhs_p[k * 2 * wide : (k + 1) * 2 * wide, :], wt_p, sums, k * wide, wide)

            for i, turn in enumerate(group):

                def keep_b(tl, hp, v):
                    if turn == 0:
                        v = v + damped[tl, hp * 8 : (hp + 1) * 8, :]
                    out_b[ph, tl, rows8(xs[k][i] * 2 + hp), :] = v

                messages(sums, k * wide + i * 64, 4, row, keep_b)

            def send_b(z, y, core, x):
                pltpu.make_async_remote_copy(
                    out_b.at[ph, y * 2 + core, rows4(x * 4 + z), :],
                    recv_b.at[ph, lax.rem(my_tl, 4), my_x, rows4(my_z * 2 + lax.div(my_tl, 4)), :],
                    send_sem.at[ph, 1],
                    recv_sem.at[ph, 4],
                    device_id=device(z, y, core, x),
                    device_id_type=MESHID,
                ).start()

            sweep(send_b, group)
        pltpu.make_async_copy(
            out_b.at[ph, my_tl, rows4(my_x * 4 + my_z), :],
            recv_b.at[ph, lax.rem(my_tl, 4), my_x, rows4(my_z * 2 + lax.div(my_tl, 4)), :],
            recv_sem.at[ph, 4],
        ).start()

        errors = e2[0:120, :].reshape(N, 8, 128)

        def inertial(j):
            edge = (d2[rows8(j), :] - spread(prv, j + 96 + N)) * keep_first
            shifted = jnp.where(pos_first, edge, before(e2[rows8(j), :]))
            jv[rows8(j), :] = shifted - jnp.sum(tb[:, j] * errors, axis=0)

        loop(N, inertial, 3)

        pltpu.make_async_copy(recv_b.at[ph], recv_b.at[ph], recv_sem.at[ph, 4]).wait()

        def tables2(gp):
            parts = regroup([jnp.sum(recv_b[ph, gl, :, rows8(gp), :], axis=0) for gl in range(4)])
            for jj in range(4):
                tab2[jj, rows8(gp), :] = parts[jj]

        loop(4, tables2, 4)
        alpha = rz / scalar_of(tab2[3])
        high, low = slot8[...] // 128, slot8[...] % 128
        for j in range(N):
            v = jv[j * 8 : (j + 1) * 8, :]
            found = jnp.zeros((8, 128), F32)
            for g4 in range(8):
                src = jnp.broadcast_to(tab2[j % 4, g4 * 4 + j // 4 : g4 * 4 + j // 4 + 1, :], (8, 128))
                found = jnp.where(high == g4, jnp.take_along_axis(src, low, axis=1), found)
            at = slice(j * 8, (j + 1) * 8)
            step = alpha * d2[at, :]
            out[0, j] = out[0, j] + step
            r3[j] = r3[j] - alpha * (v + found)
        return rz

    lax.fori_loop(0, 2, phase, jnp.ones((1, 1), F32))
    out[1] = r3[...]
    for ph in range(2):
        for way in range(2):
            sent = sums.at[:, pl.ds(0, 254), :]
            pltpu.make_async_copy(sent, sent, send_sem.at[ph, way]).wait()


def finish(both, x_out, r_out, sem):
    copies = [
        pltpu.make_async_copy(both.at[n, pl.ds(0, N), a, :], dst.at[:, pl.ds(a * 128, 128)], sem.at[n, a])
        for n, dst in enumerate((x_out, r_out))
        for a in range(8)
    ]
    for copy in copies:
        copy.start()
    for copy in copies:
        copy.wait()


def on_device(right_side, transition, precond, slot_of, cluster_id, damping, pair_first, pair_second, pair_blocks):
    vm = pl.BlockSpec(memory_space=pltpu.VMEM)
    anywhere = pl.BlockSpec(memory_space=pl.ANY)
    field = pltpu.VMEM((128, 128), F32)
    whole = jnp.int32
    both = pl.pallas_call(
        kernel,
        out_shape=pltpu.VMEM((2, 16, 8, 128), F32),
        in_specs=[anywhere] * 12,
        out_specs=vm,
        scratch_shapes=[
            pltpu.VMEM((1, 1024), whole), pltpu.VMEM((8, 128), whole), pltpu.VMEM((8, 128), whole), pltpu.VMEM((1, 64), F32),
            pltpu.VMEM((1, 2048), whole), pltpu.VMEM((1, 2048), whole), pltpu.VMEM((16, 128), whole), pltpu.VMEM((16, 128), whole),
            pltpu.VMEM((N, N, 8, 128), F32),
            pltpu.VMEM((N, N, 8, 128), F32),
            pltpu.VMEM((N, N, 16, 128), F32),
            pltpu.VMEM((16, 8, 128), F32),
            field, field, field, field, field, field,
            pltpu.VMEM((N, 16, 128), F32),
            pltpu.VMEM((N, 16, 128), F32),
            pltpu.VMEM((256, 128), F32),
            pltpu.VMEM((256, 128), F32),
            pltpu.VMEM((4, 2, 64, 128), F32),
            pltpu.VMEM((4, 32, 128), F32),
            pltpu.VMEM((2, 256, 128), F32),
            pltpu.VMEM((256, 1024), BF16),
            pltpu.VMEM((64, 1024), BF16),
            pltpu.VMEM((128, 1024), BF16),
            pltpu.VMEM((256, 4096), BF16),
            pltpu.VMEM((256, 4096), BF16),
            pltpu.VMEM((2, 16, 4096), BF16),
            pltpu.VMEM((512, 4096), BF16),
            pltpu.VMEM((8, 16, 128), F32),
            pltpu.VMEM((2, 8, 16, 128), F32),
            pltpu.VMEM((2, 8, 64, 128), F32),
            pltpu.VMEM((2, 8, 64, 128), F32),
            pltpu.VMEM((2, 4, 4, 32, 128), F32),
            pltpu.SemaphoreType.DMA((5, 8)),
            pltpu.SemaphoreType.DMA((2, 2)),
            pltpu.SemaphoreType.DMA((2, 5)),
        ],
        compiler_params=pltpu.CompilerParams(collective_id=0, has_side_effects=True, vmem_limit_bytes=60 * 1024 * 1024),
    )(
        right_side,
        slot_of.reshape(1, 1024),
        slot_of.reshape(8, 128),
        cluster_id.reshape(8, 128),
        damping,
        pair_first.reshape(1, 2048),
        pair_second.reshape(1, 2048),
        pair_first.reshape(16, 128),
        pair_second.reshape(16, 128),
        precond,
        transition,
        pair_blocks.reshape(N, N, 16, 128),
    )
    return pl.pallas_call(
        finish,
        out_shape=(jax.ShapeDtypeStruct((N, 1024), F32),) * 2,
        in_specs=[vm],
        out_specs=(anywhere, anywhere),
        scratch_shapes=[pltpu.SemaphoreType.DMA((2, 8))],
    )(pltpu.with_memory_space_constraint(both, pltpu.VMEM))


def solution(mesh):
    placed = (
        P(None, ("tm", "clus")),
        P(None, None, ("tm", "clus")),
        P(None, None, ("tm", "clus")),
        P(("tm", "clus")),
        P("tm", "clus"),
        P("tm", None),
        P("tm", "clus"),
        P("tm", "clus"),
        P(None, None, "tm", "clus"),
    )
    return jax.shard_map(
        on_device,
        mesh=mesh,
        in_specs=placed,
        out_specs=(P(None, ("tm", "clus")), P(None, ("tm", "clus"))),
        check_vma=False,
    )
```

```python
import jax
import jax.numpy as jnp
from jax import lax
from jax.experimental import pallas as pl
from jax.experimental.pallas import tpu as pltpu
from jax.sharding import PartitionSpec as P

MESHID = pl.DeviceIdType.MESH
F32 = jnp.float32
BF16 = jnp.bfloat16
N = 15


def hops(d):
    return min(d, 4 - d)


OFFSETS = sorted(
    ((z, y, c, x) for z in range(4) for y in range(4) for c in range(2) for x in range(4) if z or y or c or x),
    key=lambda o: -hops(o[0]) - hops(o[1]) - hops(o[3]),
)


def place():
    tm = lax.axis_index("tm")
    return lax.div(tm, 8), lax.rem(lax.div(tm, 2), 4), lax.rem(tm, 2), lax.axis_index("clus")


def sweep(action, turns=(0, 1, 2, 3)):
    sizes = (4, 4, 2, 4)
    turned = [[lax.rem(at + d, n) for d in range(n)] for at, n in zip(place(), sizes)]
    for offset in OFFSETS:
        if offset[3] in turns:
            action(*(turned[k][d] for k, d in enumerate(offset)))


def device(z, y, core, x):
    return (z * 8 + y * 2 + core, x)


def iota(shape, axis):
    return lax.broadcasted_iota(jnp.int32, shape, axis)


def total(v):
    while v.ndim > 2:
        v = jnp.sum(v, axis=0)
    return jnp.sum(v, axis=(0, 1), keepdims=True)


def loop(n, body, unroll=1):
    def step(i, c):
        body(i)
        return c

    lax.fori_loop(0, n, step, 0, unroll=unroll)


def rows8(i):
    return pl.ds(pl.multiple_of(i * 8, 8), 8)


def rows16(i):
    return pl.ds(pl.multiple_of(i * 16, 16), 16)


def rows4(i):
    return pl.ds(pl.multiple_of(i * 4, 4), 4)


def lanes(i):
    return pl.ds(pl.multiple_of(i * 128, 128), 128)


def multiply(blocks, src, dst):
    field = src[0:N]

    def one(i):
        dst[rows8(i), :] = jnp.sum(blocks[i] * field, axis=0)

    loop(N, one, N)


def after(v):
    turned = pltpu.roll(v, 127, axis=1)
    return jnp.where(iota((8, 128), 1) == 127, pltpu.roll(turned, 7, axis=0), turned)


def before(v):
    turned = pltpu.roll(v, 1, axis=1)
    return jnp.where(iota((8, 128), 1) == 0, pltpu.roll(turned, 1, axis=0), turned)


def spread(row, j):
    return jnp.take_along_axis(jnp.broadcast_to(row, (8, 128)), jnp.full((8, 128), j, jnp.int32), axis=1)


def extras(z2, mv2, scalar):
    lane, sub = iota((16, 128), 1), iota((16, 128), 0)
    first = jnp.sum(jnp.where(lane == 0, z2[pl.ds(0, 16, stride=8), :], 0.0), axis=1, keepdims=True)
    last = jnp.sum(jnp.where(lane == 127, mv2[pl.ds(7, 16, stride=8), :], 0.0), axis=1, keepdims=True)
    row = jnp.where(lane % 32 == sub, first, 0.0) + jnp.where(lane % 32 == sub + N, last, 0.0)
    return jnp.where(iota((1, 128), 1) % 32 == 30, scalar, jnp.sum(row, axis=0, keepdims=True))


def fill(src2, stride, tiles, base, count, onehot, lhs):
    def one(a):
        v = src2[pl.ds(a, 16, stride=stride), :]
        high = v.astype(BF16)
        low = (v - high.astype(F32)).astype(BF16)
        cols = lanes(base + a)
        for n in range(count):
            mask = onehot[n * 16 : (n + 1) * 16, cols]
            lhs[n * 16 : (n + 1) * 16, cols] = high * mask
            lhs[(count + n) * 16 : (count + n + 1) * 16, cols] = low * mask

    loop(tiles, one, 2)


def spread_sum(lhs, wt, sums, base, count):
    made = lax.dot_general(lhs, wt[...], (((1,), (1,)), ((), ())), preferred_element_type=F32)
    made = made[0:count] + made[count:]
    sums[0, base : base + count, :] = made[:, 0:128]
    sums[1, base : base + count, :] = made[:, 128:256]


def messages(sums, base, count, row, store):
    for half in range(2):
        sums[half, pl.ds(base + N, count, stride=16), :] = jnp.broadcast_to(row, (count, 128))
    for hp in range(count // 2):
        for half in range(2):
            made = regroup([sums[half, pl.ds(base + hp * 32 + jj, 8, stride=4), :] for jj in range(4)])
            for tl in range(4):
                store(half * 4 + tl, hp, made[tl])


def regroup(v):
    group = iota((8, 128), 1) // 32
    low, even = group < 2, group % 2 == 0
    a = [jnp.where(low, v[i], pltpu.roll(v[i + 2], 64, axis=1)) for i in range(2)]
    a += [jnp.where(low, pltpu.roll(v[i], 64, axis=1), v[i + 2]) for i in range(2)]
    out = []
    for i in (0, 2):
        out.append(jnp.where(even, a[i], pltpu.roll(a[i + 1], 32, axis=1)))
        out.append(jnp.where(even, pltpu.roll(a[i], 96, axis=1), a[i + 1]))
    return out


def scalar_of(v):
    keep = (iota(v.shape, 0) % 4 == 3) & (iota(v.shape, 1) % 32 == 30)
    return total(jnp.where(keep, v, 0.0))


def kernel(
    b_any, slot_any, slot8_any, cid8_any, damp_any, pf_any, ps_any, pf16_any, ps16_any, m_any, t_any, blk_any,
    out,
    slot_row, slot8, cid8, damp, pf_row, ps_row, pf16, ps16,
    mb, tb, blk, r3, z2, d2, mv, ez, e2, jv, near, far, f2, b2, tab, tab2, sums,
    wt_s, oh_s, lhs_s, wt_p, oh_p, lhs_p, lam, out_f, out_b, recv_f, recv_b,
    load_sem, send_sem, recv_sem,
):
    tm = lax.axis_index("tm")
    cl = lax.axis_index("clus")
    flat = tm * 4 + cl
    my_z, my_y, my_core, my_x = place()
    my_tl = my_y * 2 + my_core
    bar = pltpu.get_barrier_semaphore()
    sweep(lambda *who: pl.semaphore_signal(bar, 1, device_id=device(*who), device_id_type=MESHID))

    def spread_load(n, src, dst):
        if len(dst.shape) == 3:
            return [
                pltpu.make_async_copy(src.at[:, pl.ds(a * 128, 128)], dst.at[pl.ds(0, N), a, :], load_sem.at[n, a]) for a in range(8)
            ]
        return [pltpu.make_async_copy(src.at[:, :, pl.ds(a * 128, 128)], dst.at[:, :, a, :], load_sem.at[n, a]) for a in range(8)]

    small = ((slot_any, slot_row), (slot8_any, slot8), (cid8_any, cid8), (damp_any, damp))
    small += ((pf_any, pf_row), (ps_any, ps_row), (pf16_any, pf16), (ps16_any, ps16))
    load_small = [pltpu.make_async_copy(src, dst, load_sem.at[3, n]) for n, (src, dst) in enumerate(small)]
    load_r, load_m, load_t = spread_load(0, b_any, r3), spread_load(1, m_any, mb), spread_load(2, t_any, tb)
    load_blk = pltpu.make_async_copy(blk_any, blk, load_sem.at[4, 0])
    for copy in load_small[:1] + load_r + load_m + load_t + load_small[1:]:
        copy.start()

    z2[120:128, :] = jnp.zeros((8, 128), F32)
    mv[120:128, :] = jnp.zeros((8, 128), F32)
    f2[240:256, :] = jnp.zeros((16, 128), F32)
    b2[240:256, :] = jnp.zeros((16, 128), F32)
    load_small[0].wait()

    def slots(a):
        index = slot_row[:, lanes(a)]
        wt_s[:, lanes(a)] = jnp.where(iota((256, 128), 0) == index % 256, 1.0, 0.0).astype(BF16)
        oh_s[:, lanes(a)] = jnp.where(iota((64, 128), 0) // 16 == index // 256, 1.0, 0.0).astype(BF16)

    loop(8, slots, 2)
    for copy in load_r:
        copy.wait()

    pos_first = (iota((8, 128), 0) == 0) & (iota((8, 128), 1) == 0)
    pos_last = (iota((8, 128), 0) == 7) & (iota((8, 128), 1) == 127)
    keep_last = jnp.where(pos_last & (flat == 127), 0.0, 1.0)
    keep_first = jnp.where(pos_first & (flat == 0), 0.0, 1.0)
    following, previous = (flat + 1) % 128, (flat + 127) % 128

    def halo(ph, who):
        return recv_f[ph, (who // 4) % 8, pl.ds(((who % 4) * 4 + who // 32) * 4 + 3, 1), :]

    out[...] = jnp.zeros_like(out)
    for field in (d2, e2, near, far):
        field[...] = jnp.zeros_like(field)

    def phase(ph, rz):
        @pl.when(ph == 0)
        def _():
            for copy in load_m:
                copy.wait()
            load_blk.start()

        multiply(mb, r3, z2)
        z3 = z2[0:120, :].reshape(N, 8, 128)
        part = total(r3[0:N] * z3)

        @pl.when(ph == 0)
        def _():
            for copy in load_t:
                copy.wait()

        multiply(tb, z3, mv)
        row = extras(z2, mv, part)
        fill(z2, 8, 8, 0, 4, oh_s, lhs_s)
        spread_sum(lhs_s[...], wt_s, sums, 0, 64)

        def keep_f(tl, hp, v):
            out_f[ph, tl, hp * 8 : (hp + 1) * 8, :] = v

        messages(sums, 0, 4, row, keep_f)

        @pl.when(ph == 0)
        def _():
            pl.semaphore_wait(bar, 127)

        def send_f(z, y, core, x):
            pltpu.make_async_remote_copy(
                out_f.at[ph, y * 2 + core, rows4(z), :],
                recv_f.at[ph, my_tl, rows4(my_x * 4 + my_z), :],
                send_sem.at[ph, 0],
                recv_sem.at[ph, my_x],
                device_id=device(z, y, core, x),
                device_id_type=MESHID,
            ).start()

        sweep(send_f)
        pltpu.make_async_copy(
            out_f.at[ph, my_tl, rows4(my_z), :], recv_f.at[ph, my_tl, rows4(my_x * 4 + my_z), :], recv_sem.at[ph, my_x]
        ).start()

        for j in range(N):
            at = slice(j * 8, (j + 1) * 8)
            ez[at, :] = jnp.where(pos_last, 0.0, after(z2[at, :])) - mv[at, :]
        @pl.when(ph == 0)
        def _():
            for copy in load_small[1:]:
                copy.wait()

            def pairs(a):
                for base, ref in ((0, pf_row), (16, ps_row)):
                    index = ref[:, lanes(a)]
                    wt_p[:, lanes(base + a)] = jnp.where(iota((256, 128), 0) == index % 256, 1.0, 0.0).astype(BF16)
                    oh_p[:, lanes(base + a)] = jnp.where(iota((256, 128), 0) // 16 == index // 256, 1.0, 0.0).astype(BF16)

            loop(16, pairs, 2)
            per = jnp.take_along_axis(jnp.broadcast_to(jnp.concatenate([damp[...]] * 2, axis=1), (8, 128)), cid8[...], axis=1)
            group = iota((8, 128), 1) // 32
            spare = (iota((4, 128), 0) == 3) & (iota((4, 128), 1) >= 96)
            for tl in range(4):
                wide = None
                for jj in range(4):
                    turn = ((jj - tl) % 4) * 32
                    moved = pltpu.roll(per, turn, axis=1) if turn else per
                    wide = moved if jj == 0 else jnp.where(group == jj, moved, wide)
                for t4 in range(8):
                    th, h = t4 // 2, t4 % 2
                    lam[h * 4 + tl, th * 4 : (th + 1) * 4, :] = jnp.where(spare, 0.0, jnp.broadcast_to(wide[t4 : t4 + 1, :], (4, 128)))
            load_blk.wait()

        for c in range(4):
            block = recv_f.at[ph, :, c * 16 : (c + 1) * 16, :]
            pltpu.make_async_copy(block, block, recv_sem.at[ph, c]).wait()

        def tables(hp):
            for h in range(2):
                parts = regroup([recv_f[ph, h * 4 + tl, rows8(hp), :] for tl in range(4)])
                for jj in range(4):
                    tab[jj, h, rows8(hp), :] = parts[jj]

        loop(8, tables, 8)
        rz_new = scalar_of(tab[3, 0]) + scalar_of(tab[3, 1])
        beta = jnp.where(ph == 0, 0.0, rz_new / rz)
        rz = rz_new
        nxt = halo(ph, following)
        prv = halo(ph, previous) + beta * halo(0, previous)
        d2[...] = z2[...] + beta * d2[...]
        part = jnp.zeros((8, 128), F32)
        for j in range(N):
            at = slice(j * 8, (j + 1) * 8)
            v = (ez[at, :] + jnp.where(pos_last, spread(nxt, j + 96), 0.0)) * keep_last
            v = v + beta * e2[at, :]
            e2[at, :] = v
            part = part + v * v
        part = total(part)

        for index16, field in ((pf16, near), (ps16, far)):
            index = [index16[pv * 8 : (pv + 1) * 8, :] for pv in range(2)]
            high = [v // 128 for v in index]
            low = [v % 128 for v in index]

            def look(quad, carry):
                carry = list(carry)
                for low_hi in range(4):
                    for h in range(2):
                        here = [v == quad * 8 + low_hi * 2 + h for v in high]
                        for j in range(N):
                            row = tab[j % 4, h, pl.ds(quad * 16 + low_hi * 4 + j // 4, 1), :]
                            src = jnp.broadcast_to(row, (8, 128))
                            for pv in range(2):
                                k = j * 2 + pv
                                carry[k] = jnp.where(here[pv], jnp.take_along_axis(src, low[pv], axis=1), carry[k])
                return tuple(carry)

            found = lax.fori_loop(0, 4, look, tuple(jnp.zeros((8, 128), F32) for _ in range(30)), unroll=2)
            for j in range(N):
                for pv in range(2):
                    v = found[j * 2 + pv]
                    v = v + beta * field[j, pv * 8 : (pv + 1) * 8, :]
                    field[j, pv * 8 : (pv + 1) * 8, :] = v

        def forward(i):
            f2[rows16(i), :] = near[i] - jnp.sum(blk[i] * far[...], axis=0)

        loop(N, forward, N)

        def backward(j):
            b2[rows16(j), :] = -jnp.sum(blk[:, j] * f2[0:240, :].reshape(N, 16, 128), axis=0)

        loop(N, backward, N)
        own = recv_f[ph, :, rows16(cl), :] + beta * recv_f[0, :, rows16(cl), :]
        damped = own * lam[...]
        part = part + total((f2[0:240, :] * f2[0:240, :]).reshape(N, 16, 128)) + total(damped * own)
        row = jnp.where(iota((1, 128), 1) % 32 == 30, part, 0.0)
        for a in range(32):
            cols = slice(a * 128, (a + 1) * 128)
            v = (f2, b2)[a // 16][pl.ds(a % 16, 16, stride=16), :]
            high = v.astype(BF16)
            both = (high, (v - high.astype(F32)).astype(BF16))
            for n in range(16):
                mask = oh_p[n * 16 : (n + 1) * 16, cols]
                for m in range(2):
                    lhs_p[m * 256 + n * 16 : m * 256 + (n + 1) * 16, cols] = both[m] * mask
        spread_sum(lhs_p[...], wt_p, sums, 0, 256)

        def keep_b(tl, hp, v):
            out_b[ph, tl, hp * 8 : (hp + 1) * 8, :] = v

        messages(sums, 0, 16, row, keep_b)
        out_b[ph, :, rows16(my_x), :] = out_b[ph, :, rows16(my_x), :] + damped

        def send_b(z, y, core, x):
            pltpu.make_async_remote_copy(
                out_b.at[ph, y * 2 + core, rows4(x * 4 + z), :],
                recv_b.at[ph, lax.rem(my_tl, 4), my_x, rows4(my_z * 2 + lax.div(my_tl, 4)), :],
                send_sem.at[ph, 1],
                recv_sem.at[ph, 4],
                device_id=device(z, y, core, x),
                device_id_type=MESHID,
            ).start()

        sweep(send_b)
        pltpu.make_async_copy(
            out_b.at[ph, my_tl, rows4(my_x * 4 + my_z), :],
            recv_b.at[ph, lax.rem(my_tl, 4), my_x, rows4(my_z * 2 + lax.div(my_tl, 4)), :],
            recv_sem.at[ph, 4],
        ).start()

        errors = e2[0:120, :].reshape(N, 8, 128)

        def inertial(j):
            edge = (d2[rows8(j), :] - spread(prv, j + 96 + N)) * keep_first
            shifted = jnp.where(pos_first, edge, before(e2[rows8(j), :]))
            jv[rows8(j), :] = shifted - jnp.sum(tb[:, j] * errors, axis=0)

        loop(N, inertial, 3)

        pltpu.make_async_copy(recv_b.at[ph], recv_b.at[ph], recv_sem.at[ph, 4]).wait()

        def tables2(gp):
            parts = regroup([jnp.sum(recv_b[ph, gl, :, rows8(gp), :], axis=0) for gl in range(4)])
            for jj in range(4):
                tab2[jj, rows8(gp), :] = parts[jj]

        loop(4, tables2, 4)
        alpha = rz / scalar_of(tab2[3])
        high, low = slot8[...] // 128, slot8[...] % 128
        for j in range(N):
            v = jv[j * 8 : (j + 1) * 8, :]
            found = jnp.zeros((8, 128), F32)
            for g4 in range(8):
                src = jnp.broadcast_to(tab2[j % 4, g4 * 4 + j // 4 : g4 * 4 + j // 4 + 1, :], (8, 128))
                found = jnp.where(high == g4, jnp.take_along_axis(src, low, axis=1), found)
            at = slice(j * 8, (j + 1) * 8)
            step = alpha * d2[at, :]
            out[0, j] = out[0, j] + step
            r3[j] = r3[j] - alpha * (v + found)
        return rz

    lax.fori_loop(0, 2, phase, jnp.ones((1, 1), F32))
    out[1] = r3[...]
    for ph in range(2):
        for way in range(2):
            sent = sums.at[:, pl.ds(0, 254), :]
            pltpu.make_async_copy(sent, sent, send_sem.at[ph, way]).wait()


def finish(both, x_out, r_out, sem):
    copies = [
        pltpu.make_async_copy(both.at[n, pl.ds(0, N), a, :], dst.at[:, pl.ds(a * 128, 128)], sem.at[n, a])
        for n, dst in enumerate((x_out, r_out))
        for a in range(8)
    ]
    for copy in copies:
        copy.start()
    for copy in copies:
        copy.wait()


def on_device(right_side, transition, precond, slot_of, cluster_id, damping, pair_first, pair_second, pair_blocks):
    vm = pl.BlockSpec(memory_space=pltpu.VMEM)
    anywhere = pl.BlockSpec(memory_space=pl.ANY)
    field = pltpu.VMEM((128, 128), F32)
    whole = jnp.int32
    both = pl.pallas_call(
        kernel,
        out_shape=pltpu.VMEM((2, 16, 8, 128), F32),
        in_specs=[anywhere] * 12,
        out_specs=vm,
        scratch_shapes=[
            pltpu.VMEM((1, 1024), whole), pltpu.VMEM((8, 128), whole), pltpu.VMEM((8, 128), whole), pltpu.VMEM((1, 64), F32),
            pltpu.VMEM((1, 2048), whole), pltpu.VMEM((1, 2048), whole), pltpu.VMEM((16, 128), whole), pltpu.VMEM((16, 128), whole),
            pltpu.VMEM((N, N, 8, 128), F32),
            pltpu.VMEM((N, N, 8, 128), F32),
            pltpu.VMEM((N, N, 16, 128), F32),
            pltpu.VMEM((16, 8, 128), F32),
            field, field, field, field, field, field,
            pltpu.VMEM((N, 16, 128), F32),
            pltpu.VMEM((N, 16, 128), F32),
            pltpu.VMEM((256, 128), F32),
            pltpu.VMEM((256, 128), F32),
            pltpu.VMEM((4, 2, 64, 128), F32),
            pltpu.VMEM((4, 32, 128), F32),
            pltpu.VMEM((2, 256, 128), F32),
            pltpu.VMEM((256, 1024), BF16),
            pltpu.VMEM((64, 1024), BF16),
            pltpu.VMEM((128, 1024), BF16),
            pltpu.VMEM((256, 4096), BF16),
            pltpu.VMEM((256, 4096), BF16),
            pltpu.VMEM((512, 4096), BF16),
            pltpu.VMEM((8, 16, 128), F32),
            pltpu.VMEM((2, 8, 16, 128), F32),
            pltpu.VMEM((2, 8, 64, 128), F32),
            pltpu.VMEM((2, 8, 64, 128), F32),
            pltpu.VMEM((2, 4, 4, 32, 128), F32),
            pltpu.SemaphoreType.DMA((5, 8)),
            pltpu.SemaphoreType.DMA((2, 2)),
            pltpu.SemaphoreType.DMA((2, 5)),
        ],
        compiler_params=pltpu.CompilerParams(collective_id=0, has_side_effects=True, vmem_limit_bytes=60 * 1024 * 1024),
    )(
        right_side,
        slot_of.reshape(1, 1024),
        slot_of.reshape(8, 128),
        cluster_id.reshape(8, 128),
        damping,
        pair_first.reshape(1, 2048),
        pair_second.reshape(1, 2048),
        pair_first.reshape(16, 128),
        pair_second.reshape(16, 128),
        precond,
        transition,
        pair_blocks.reshape(N, N, 16, 128),
    )
    return pl.pallas_call(
        finish,
        out_shape=(jax.ShapeDtypeStruct((N, 1024), F32),) * 2,
        in_specs=[vm],
        out_specs=(anywhere, anywhere),
        scratch_shapes=[pltpu.SemaphoreType.DMA((2, 8))],
    )(pltpu.with_memory_space_constraint(both, pltpu.VMEM))


def solution(mesh):
    placed = (
        P(None, ("tm", "clus")),
        P(None, None, ("tm", "clus")),
        P(None, None, ("tm", "clus")),
        P(("tm", "clus")),
        P("tm", "clus"),
        P("tm", None),
        P("tm", "clus"),
        P("tm", "clus"),
        P(None, None, "tm", "clus"),
    )
    return jax.shard_map(
        on_device,
        mesh=mesh,
        in_specs=placed,
        out_specs=(P(None, ("tm", "clus")), P(None, ("tm", "clus"))),
        check_vma=False,
    )
```
